256 devices in a mesh: gx: 4 (over y), gy: 4 (over x_lo, core), gz: 16 (over z, x_hi).
Axes of the slice: x: 4 (x_hi: 2, x_lo: 2; x = x_hi * 2 + x_lo), y: 4, z: 8, core: 2. Of those that a mesh axis runs over, the one named last changes fastest.
Arguments:
- phases: float32 [16, 16, 16, 96, 256], P('gx', 'gy', 'gz'), may hold values from -3.140625 to 3.140625
- diag_tiles: float32 [16, 16, 16, 96, 96], P('gx', 'gy', 'gz'), may hold values from -0.078125 to 0.078125
- local_tiles: float32 [4, 4, 16, 48, 96, 96], P('gx', 'gy', 'gz'), may hold values from -0.078125 to 0.078125
- local_pairs: int32 [4, 4, 16, 2, 48], P('gx', 'gy', 'gz'), may hold values from 0 to 15
- face_tiles: float32 [4, 4, 16, 2, 8, 96, 96], P('gx', 'gy', 'gz'), may hold values from -0.078125 to 0.078125
- face_pairs: int32 [4, 4, 16, 2, 2, 8], P('gx', 'gy', 'gz'), may hold values from 0 to 3
- layer_tiles: float32 [4, 4, 16, 32, 96, 96], P('gx', 'gy', 'gz'), may hold values from -0.078125 to 0.078125
- layer_pairs: int32 [4, 4, 16, 2, 32], P('gx', 'gy', 'gz'), may hold values from 0 to 15
Outputs:
- order_three: float32 [16, 16, 16, 96, 256], P('gx', 'gy', 'gz')
- moments: float32 [16, 7, 256], P('gz')
The draws below stay inside these ranges and needn't reach their ends.
Inputs may be any that keep to these rules, and one draw needn't show every extreme that they name: `local_pairs`: local pairs may repeat and may name one cluster twice. `face_pairs`: face slots number clusters along the face.
All inputs are finite; a program needn't handle non-finite values.
Results may differ from the reference program's by a relative error of at most 0.00005.
Values sent between devices are 32-bit elements; how exact they have to be, the bound alone decides.
No kernel may reach another device: no remote copies, remote signals or barrier semaphores. Data moves between devices by JAX's collectives and lax.ppermute only.
A program may use at most 128 MiB of HBM per device.

```python
import math
import jax
import jax.numpy as jnp
from jax import lax

DOF = 96
COLS = 256
SIDE = 4
LOCAL = 48
FACE = 8
LAYER = 32
NX = 16
NY = 16
NZ = 16
N_GX = 4
N_GY = 4
N_GZ = 16


def set_ends(values, key, smallest, top_value):
    longest = values.shape.index(max(values.shape))
    spots = []
    for shift in (0, 1):
        where = [jax.random.randint(jax.random.fold_in(key, axis), (), 0, length) for axis, length in enumerate(values.shape)]
        where[longest] = (where[longest] + shift) % values.shape[longest]
        spots.append(tuple(where))
    return values.at[spots[0]].set(smallest).at[spots[1]].set(top_value)


def levels(stream_key, extent, shards, least, high):
    gain, own = 1.0, jax.random.fold_in(stream_key, 6)
    for position, shards_of in shards:
        steps = jnp.exp(jax.random.uniform(jax.random.fold_in(own, position), (shards_of,), jnp.float32, least / len(shards), high / len(shards)))
        gain = gain * jnp.repeat(steps, extent[position] // shards_of).reshape([-1 if axis == position else 1 for axis in range(len(extent))])
    return gain


def centred(own_key, extent, width, most, split=(), kind=jnp.bfloat16):
    values = jax.random.normal(own_key, extent, jnp.float32) * width
    if len(split) > 0:
        values = levels(own_key, extent, split, -0.22, 0.18) * values
    return jnp.clip(values, min=-most, max=most).astype(kind)


def setup_inputs(seed: int = 0) -> dict:
    seeds = jax.random.split(jax.random.key(seed), 9)
    phases = jnp.clip(jax.random.uniform(seeds[0], (NX, NY, NZ, DOF, COLS), jnp.float32, -3.140625, 3.140625), -3.140625, 3.140625)
    diag_tiles = centred(seeds[1], (NX, NY, NZ, DOF, DOF), (64 * DOF) ** -0.5, 0.078125, ((0, 4), (1, 4), (2, 16)), jnp.float32)
    local_tiles = centred(seeds[2], (N_GX, N_GY, N_GZ, LOCAL, DOF, DOF), (64 * DOF) ** -0.5, 0.078125, ((0, 4), (1, 4), (2, 16)), jnp.float32)
    local_pairs = set_ends(jax.random.randint(seeds[3], (N_GX, N_GY, N_GZ, 2, LOCAL), 0, SIDE * SIDE), jax.random.fold_in(seeds[3], 1), 0, (SIDE * SIDE) - 1).astype(jnp.int32)
    face_tiles = centred(seeds[4], (N_GX, N_GY, N_GZ, 2, FACE, DOF, DOF), (64 * DOF) ** -0.5, 0.078125, ((0, 4), (1, 4), (2, 16)), jnp.float32)
    face_pairs = set_ends(jax.random.randint(seeds[5], (N_GX, N_GY, N_GZ, 2, 2, FACE), 0, SIDE), jax.random.fold_in(seeds[5], 1), 0, SIDE - 1).astype(jnp.int32)
    layer_tiles = centred(seeds[6], (N_GX, N_GY, N_GZ, LAYER, DOF, DOF), (64 * DOF) ** -0.5, 0.078125, ((0, 4), (1, 4), (2, 16)), jnp.float32)
    layer_pairs = set_ends(jax.random.randint(seeds[7], (N_GX, N_GY, N_GZ, 2, LAYER), 0, SIDE * SIDE), jax.random.fold_in(seeds[7], 1), 0, (SIDE * SIDE) - 1).astype(jnp.int32)
    return dict(phases=phases, diag_tiles=diag_tiles, local_tiles=local_tiles, local_pairs=local_pairs, face_tiles=face_tiles, face_pairs=face_pairs, layer_tiles=layer_tiles, layer_pairs=layer_pairs)


TOP_PRECISION = lax.Precision.HIGHEST

def to_bricks(field, trailing):
    shaped = field.reshape((N_GX, SIDE, N_GY, SIDE, N_GZ) + trailing)
    return shaped.transpose(0, 2, 4, 1, 3, 5, 6)

def from_bricks(bricks):
    return bricks.transpose(0, 3, 1, 4, 2, 5, 6).reshape(N_GX * SIDE, N_GY * SIDE, N_GZ, DOF, COLS)

def pair_terms(packed):
    tile_set, pair_list, owner_site_vectors, partner_site_vectors = packed
    forward = jnp.einsum('kab,kbr->kar', tile_set, partner_site_vectors[pair_list[1]], precision=TOP_PRECISION)
    backward = jnp.einsum('kba,kbr->kar', tile_set, owner_site_vectors[pair_list[0]], precision=TOP_PRECISION)
    owner_add = jnp.zeros_like(owner_site_vectors).at[pair_list[0]].add(forward)
    partner_add = jnp.zeros_like(partner_site_vectors).at[pair_list[1]].add(backward)
    return (owner_add, partner_add)

def mapped(tile_set, pair_list, owner_site_vectors, partner_site_vectors):
    brick_count = N_GX * N_GY * N_GZ
    packed = (tile_set.reshape((brick_count,) + tile_set.shape[3:]), pair_list.reshape((brick_count,) + pair_list.shape[3:]), owner_site_vectors.reshape((brick_count,) + owner_site_vectors.shape[3:]), partner_site_vectors.reshape((brick_count,) + partner_site_vectors.shape[3:]))
    owner_add, partner_add = lax.map(pair_terms, packed)
    return (owner_add.reshape(owner_site_vectors.shape), partner_add.reshape(partner_site_vectors.shape))

def operate(field, diag_tiles, local_tiles, local_pairs, face_tiles, face_pairs, layer_tiles, layer_pairs):
    bricks = to_bricks(field, (DOF, COLS))
    diagonal = to_bricks(diag_tiles, (DOF, DOF))
    symmetric = diagonal + jnp.swapaxes(diagonal, 5, 6)
    result = jnp.einsum('ghipqab,ghipqbr->ghipqar', symmetric, bricks, precision=TOP_PRECISION)
    flat = bricks.reshape(N_GX, N_GY, N_GZ, SIDE * SIDE, DOF, COLS)
    owner_add, partner_add = mapped(local_tiles, local_pairs, flat, flat)
    result = result + (owner_add + partner_add).reshape(bricks.shape)
    upper = bricks[:, :, :, SIDE - 1]
    lower = jnp.roll(bricks[:, :, :, 0], -1, axis=0)
    owner_add, partner_add = mapped(face_tiles[:, :, :, 0], face_pairs[:, :, :, 0], upper, lower)
    result = result.at[:, :, :, SIDE - 1].add(owner_add)
    result = result.at[:, :, :, 0].add(jnp.roll(partner_add, 1, axis=0))
    upper = bricks[:, :, :, :, SIDE - 1]
    lower = jnp.roll(bricks[:, :, :, :, 0], -1, axis=1)
    owner_add, partner_add = mapped(face_tiles[:, :, :, 1], face_pairs[:, :, :, 1], upper, lower)
    result = result.at[:, :, :, :, SIDE - 1].add(owner_add)
    result = result.at[:, :, :, :, 0].add(jnp.roll(partner_add, 1, axis=1))
    above = jnp.roll(flat, -1, axis=2)
    owner_add, partner_add = mapped(layer_tiles, layer_pairs, flat, above)
    result = result + (owner_add + jnp.roll(partner_add, 1, axis=2)).reshape(bricks.shape)
    return from_bricks(result)

def product(left_vec, right_vec):
    return lax.optimization_barrier(jnp.sum(left_vec * right_vec, axis=(0, 1, 3)))

def reference(phases, diag_tiles, local_tiles, local_pairs, face_tiles, face_pairs, layer_tiles, layer_pairs):
    lookup_tables = (diag_tiles, local_tiles, local_pairs, face_tiles, face_pairs, layer_tiles, layer_pairs)
    initial = math.sqrt(2.0) * jnp.cos(phases)
    order_one = operate(initial, *lookup_tables)
    order_two = 2.0 * operate(order_one, *lookup_tables) - initial
    order_three = 2.0 * operate(order_two, *lookup_tables) - order_one
    partials = [product(initial, initial), product(initial, order_one), product(order_one, order_one), product(order_two, order_one), product(order_two, order_two), product(order_three, order_two), product(order_three, order_three)]
    stacked = jnp.stack([partials[0], partials[1], 2.0 * partials[2] - partials[0], 2.0 * partials[3] - partials[1], 2.0 * partials[4] - partials[0], 2.0 * partials[5] - partials[1], 2.0 * partials[6] - partials[0]], axis=1)
    moments = stacked / (N_GX * SIDE * N_GY * SIDE * DOF)
    return (order_three, moments)
```

```python
import functools
import math

import jax
import jax.numpy as jnp
from jax import lax
from jax.experimental import pallas as pl
from jax.experimental.pallas import tpu as pltpu
from jax.sharding import PartitionSpec as P


D = 96
R = 256
E = 4
C = 16
N = C * D
G = E * D
F32 = jnp.float32
BF16 = jnp.bfloat16


def vmem():
    return pl.BlockSpec(memory_space=pltpu.VMEM)


def smem():
    return pl.BlockSpec(memory_space=pltpu.SMEM)


def whole(shape):
    zeros = (0,) * len(shape)
    return pl.BlockSpec(shape, lambda *_: zeros)


def split(x):
    hi = x.astype(BF16)
    return hi, (x - hi.astype(F32)).astype(BF16)


def dot(a, b):
    return jnp.dot(a, b, preferred_element_type=F32)


def dot3(ah, al, bh, bl):
    return dot(ah, bh) + (dot(ah, bl) + dot(al, bh))


def cosine(x):
    turns = jnp.floor(x * (0.5 / math.pi) + 0.5)
    x = x - turns * (2.0 * math.pi)
    y = x * 0.5
    t = y * y
    s = t * (-1.0 / 39916800.0) + (1.0 / 362880.0)
    s = s * t + (-1.0 / 5040.0)
    s = s * t + (1.0 / 120.0)
    s = s * t + (-1.0 / 6.0)
    s = y + y * t * s
    return 1.0 - 2.0 * s * s


def colsum(x):
    return jnp.sum(x, axis=0, keepdims=True)


def initial_body(ph, p0, p1, p2, p3, south, north, mom):
    total = jnp.zeros((1, R), F32)
    for i, out in enumerate((p0, p1, p2, p3)):
        for j in range(E):
            v = math.sqrt(2.0) * cosine(ph[i, j])
            out[j] = v
            if j == 0:
                south[i] = v
            if j == E - 1:
                north[i] = v
            total = total + colsum(v * v)
    mom[...] = total


def initial_vectors(phases):
    piece = jax.ShapeDtypeStruct((E, D, R), F32)
    return pl.pallas_call(
        initial_body,
        out_shape=(piece,) * 6 + (jax.ShapeDtypeStruct((1, R), F32),),
        in_specs=[vmem()],
        out_specs=(vmem(),) * 7,
        cost_estimate=pl.CostEstimate(flops=30 * N * R, bytes_accessed=4 * N * R * 3, transcendentals=0),
        name="initial",
    )(phases)


def pack_body(layer, face, lp, xp, yp):
    def quad(src, dst, j):
        last = src(4 * j + 3)
        for i in range(3):
            dst[3 * j + i, :, 0:D] = src(4 * j + i)
            dst[3 * j + i, :, D:128] = last[:, 32 * i : 32 * i + 32]

    for j in range(8):
        quad(lambda k: layer[k], lp, j)
    for j in range(2):
        quad(lambda k: face[0, k], xp, j)
        quad(lambda k: face[1, k], yp, j)


def pack(layer, face):
    def out(n):
        return jax.ShapeDtypeStruct((n, D, 128), F32)

    return pl.pallas_call(
        pack_body,
        out_shape=(out(24), out(6), out(6)),
        in_specs=[vmem()] * 2,
        out_specs=(vmem(),) * 3,
        cost_estimate=pl.CostEstimate(flops=0, bytes_accessed=4 * 48 * D * 256, transcendentals=0),
        name="pack",
    )(layer, face)


def unpacked(ref, j, i):
    if i < 3:
        return ref[3 * j + i, :, 0:D]
    parts = [ref[3 * j + n, :, D:128] for n in range(3)]
    return jnp.concatenate(parts, axis=1)


def accumulate(acc, row, col, tile):
    group = lax.shift_right_logical(col, 2)
    place = lax.bitwise_and(col, 3)
    rows = pl.ds(pl.multiple_of(row * D, 8), D)
    for j in range(4):

        @pl.when(place == j)
        def _():
            at = (group, rows, slice(D * j, D * j + D))
            acc[at] = acc[at] + tile


def clear(acc):
    def step(i, carry):
        rows = pl.ds(pl.multiple_of(i * D, 8), D)
        for g in range(4):
            acc[g, rows, :] = jnp.zeros((D, G), F32)
        return carry

    lax.fori_loop(0, C, step, 0)


def local_body(pairs, diag, tiles, hi, lo, acc):
    m = pl.program_id(0)

    @pl.when(m == 0)
    def _():
        clear(acc)
        for c in range(C):
            t = diag[c]
            acc[c // 4, D * c : D * c + D, D * (c % 4) : D * (c % 4) + D] = t + t.T

        def step(k, carry):
            o = pairs[0, k]
            p = pairs[1, k]
            t = tiles[k]
            accumulate(acc, o, p, t)
            accumulate(acc, p, o, t.T)
            return carry

        lax.fori_loop(0, 48, step, 0)

    emit(acc, m, hi, lo)


def emit(acc, m, hi, lo):
    for i in range(E):
        rows = pl.ds(pl.multiple_of(m * G + i * D, 8), D)
        for g in range(4):
            h, l = split(acc[g, rows, :])
            at = (slice(D * i, D * i + D), slice(G * g, G * g + G))
            hi[at] = h
            lo[at] = l


def local_operator(pairs, diag, tiles):
    out = jax.ShapeDtypeStruct((N, N), BF16)
    spec = pl.BlockSpec((G, N), lambda m: (m, 0))
    return pl.pallas_call(
        local_body,
        grid=(4,),
        out_shape=(out, out),
        in_specs=[smem(), whole((C, D, D)), whole((48, D, D))],
        out_specs=(spec, spec),
        scratch_shapes=[pltpu.VMEM((4, N, G), F32)],
        cost_estimate=pl.CostEstimate(flops=30 * N * N, bytes_accessed=8 * N * N, transcendentals=0),
        name="local_operator",
    )(pairs, diag, tiles)


def layer_body(odd, own_pairs, low_pairs, own, low, hi, lo, acc):
    slot = pl.program_id(0)
    m = pl.program_id(1)
    mine = slot == odd[0]

    @pl.when(m == 0)
    def _():
        clear(acc)

        @pl.when(mine)
        def _():
            def step(k, carry):
                accumulate(acc, own_pairs[0, k], own_pairs[1, k], own[k])
                return carry

            lax.fori_loop(0, 32, step, 0)

        @pl.when(jnp.logical_not(mine))
        def _():
            def step(j, carry):
                for i in range(4):
                    k = 4 * j + i
                    accumulate(acc, low_pairs[1, k], low_pairs[0, k], unpacked(low, j, i).T)
                return carry

            lax.fori_loop(0, 8, step, 0)

    emit(acc, m, hi.at[0], lo.at[0])


def layer_operators(odd, own_pairs, low_pairs, own, low):
    out = jax.ShapeDtypeStruct((2, N, N), BF16)
    spec = pl.BlockSpec((1, G, N), lambda s, m: (s, m, 0))
    return pl.pallas_call(
        layer_body,
        grid=(2, 4),
        out_shape=(out, out),
        in_specs=[smem(), smem(), smem(), whole((32, D, D)), whole((24, D, 128))],
        out_specs=(spec, spec),
        scratch_shapes=[pltpu.VMEM((4, N, G), F32)],
        cost_estimate=pl.CostEstimate(flops=50 * N * N, bytes_accessed=16 * N * N, transcendentals=0),
        name="layer_operators",
    )(odd, own_pairs, low_pairs, own, low)


def face_op_body(pairs, west_pairs, south_pairs, face, west, south, hi, lo, acc):
    for i in range(4):
        acc[i] = jnp.zeros((G, G), F32)

    def add(i, row, col, tile):
        rows = pl.ds(pl.multiple_of(row * D, 8), D)
        for j in range(4):

            @pl.when(col == j)
            def _():
                at = (i, rows, slice(D * j, D * j + D))
                acc[at] = acc[at] + tile

    for k in range(8):
        add(0, pairs[0, 0, k], pairs[0, 1, k], face[0, k])
        add(1, west_pairs[1, k], west_pairs[0, k], unpacked(west, k // 4, k % 4).T)
        add(2, pairs[1, 0, k], pairs[1, 1, k], face[1, k])
        add(3, south_pairs[1, k], south_pairs[0, k], unpacked(south, k // 4, k % 4).T)
    for i in range(4):
        h, l = split(acc[i])
        hi[i] = h
        lo[i] = l


def face_operators(pairs, west_pairs, south_pairs, face, west, south):
    out = jax.ShapeDtypeStruct((4, G, G), BF16)
    return pl.pallas_call(
        face_op_body,
        out_shape=(out, out),
        in_specs=[smem()] * 3 + [vmem()] * 3,
        out_specs=(vmem(), vmem()),
        scratch_shapes=[pltpu.VMEM((4, G, G), F32)],
        cost_estimate=pl.CostEstimate(flops=40 * G * G, bytes_accessed=32 * G * G, transcendentals=0),
        name="face_operators",
    )(pairs, west_pairs, south_pairs, face, west, south)


def load_pieces(pieces, vh, vl):
    for i, piece in enumerate(pieces):
        h, l = split(piece[...].reshape(G, R))
        vh[G * i : G * i + G, :] = h
        vl[G * i : G * i + G, :] = l


def product_body(first, *refs):
    if first:
        hi, lo, p0, p1, p2, p3, out, vh, vl = refs
        acc = None
    else:
        hi, lo, p0, p1, p2, p3, acc, out, vh, vl = refs

    @pl.when(pl.program_id(0) == 0)
    def _():
        load_pieces((p0, p1, p2, p3), vh, vl)

    a, b = (hi[...], lo[...]) if first else (hi[0], lo[0])
    r = dot3(a, b, vh[...], vl[...])
    out[...] = r if first else acc[...] + r


PRODUCT_COST = pl.CostEstimate(flops=6 * N * N * R, bytes_accessed=4 * N * N + 12 * N * R, transcendentals=0)


def apply_local(ops, pieces):
    spec = pl.BlockSpec((G, N), lambda m: (m, 0))
    return pl.pallas_call(
        functools.partial(product_body, True),
        grid=(4,),
        out_shape=jax.ShapeDtypeStruct((N, R), F32),
        in_specs=[spec, spec] + [whole((E, D, R))] * 4,
        out_specs=pl.BlockSpec((G, R), lambda m: (m, 0)),
        scratch_shapes=[pltpu.VMEM((N, R), BF16)] * 2,
        cost_estimate=PRODUCT_COST,
        name="apply_local",
    )(*ops, *pieces)


def apply_across(ops, pieces, acc):
    spec = pl.BlockSpec((1, G, N), lambda m: (0, m, 0))
    rows = pl.BlockSpec((G, R), lambda m: (m, 0))
    return pl.pallas_call(
        functools.partial(product_body, False),
        grid=(4,),
        out_shape=jax.ShapeDtypeStruct((N, R), F32),
        in_specs=[spec, spec] + [whole((E, D, R))] * 4 + [rows],
        out_specs=rows,
        scratch_shapes=[pltpu.VMEM((N, R), BF16)] * 2,
        cost_estimate=PRODUCT_COST,
        name="apply_across",
    )(*ops, *pieces, acc)


def faces_body(hi, lo, east, west, north, south, acc, out):
    out[...] = acc[...]

    def term(i, v):
        h, l = split(v[...].reshape(G, R))
        return dot3(hi[i], lo[i], h, l)

    out[G * 3 : G * 4, :] += term(0, east)
    out[0:G, :] += term(1, west)
    t = term(2, north)
    u = term(3, south)
    for s in range(E):
        out[G * s + 3 * D : G * s + G, :] += t[D * s : D * s + D]
        out[G * s : G * s + D, :] += u[D * s : D * s + D]


def apply_faces(ops, east, west, north, south, acc):
    return pl.pallas_call(
        faces_body,
        out_shape=jax.ShapeDtypeStruct((N, R), F32),
        in_specs=[vmem()] * 7,
        out_specs=vmem(),
        cost_estimate=pl.CostEstimate(flops=24 * G * G * R, bytes_accessed=8 * N * R + 16 * G * G, transcendentals=0),
        name="apply_faces",
    )(*ops, east, west, north, south, acc)


def finish_body(scale, with_prev, last, *refs):
    refs = list(refs)
    hi, lo = refs[:2]
    z = refs[2:6]
    acc = refs[6]
    now = refs[7:11]
    refs = refs[11:]
    prev = None
    if with_prev:
        prev, refs = refs[:4], refs[4:]
    if last:
        full, mom, vh, vl = refs
    else:
        outs, (south, north, mom, vh, vl) = refs[:4], refs[4:]
    m = pl.program_id(0)

    @pl.when(m == 0)
    def _():
        load_pieces(z, vh, vl)
        mom[...] = jnp.zeros((2, R), F32)

    r = acc[...] + dot3(hi[0], lo[0], vh[...], vl[...])
    if scale != 1.0:
        r = scale * r
    for i in range(4):

        @pl.when(m == i)
        def _():
            v = now[i][...].reshape(G, R)
            w = r
            if with_prev:
                w = w - prev[i][...].reshape(G, R)
            mom[0:1, :] += colsum(w * v)
            mom[1:2, :] += colsum(w * w)
            w = w.reshape(E, D, R)
            if last:
                full[...] = w
            else:
                outs[i][...] = w
                south[i] = w[0]
                north[i] = w[E - 1]


def finish(ops, z, acc, now, prev, scale, last):
    spec = pl.BlockSpec((1, G, N), lambda m: (1, m, 0))
    rows = pl.BlockSpec((G, R), lambda m: (m, 0))
    piece = jax.ShapeDtypeStruct((E, D, R), F32)
    moment = jax.ShapeDtypeStruct((2, R), F32)
    block = whole((E, D, R))
    args = [*ops, *z, acc, *now]
    in_specs = [spec, spec] + [block] * 4 + [rows] + [block] * 4
    if prev is not None:
        args += [*prev]
        in_specs += [block] * 4
    if last:
        out_shape = (jax.ShapeDtypeStruct((C, D, R), F32), moment)
        out_specs = (pl.BlockSpec((E, D, R), lambda m: (m, 0, 0)), whole((2, R)))
    else:
        out_shape = (piece,) * 6 + (moment,)
        out_specs = (block,) * 6 + (whole((2, R)),)
    return pl.pallas_call(
        functools.partial(finish_body, scale, prev is not None, last),
        grid=(4,),
        out_shape=out_shape,
        in_specs=in_specs,
        out_specs=out_specs,
        scratch_shapes=[pltpu.VMEM((N, R), BF16)] * 2,
        cost_estimate=PRODUCT_COST,
        name="finish",
    )(*args)


def shift(x, axis, distance):
    n = lax.axis_size(axis)
    return lax.ppermute(x, axis, [(i, (i + distance) % n) for i in range(n)])


def across(x):
    n = lax.axis_size("gz")
    return lax.ppermute(x, "gz", [(i, i ^ 1) for i in range(n)])


def forward(x):
    n = lax.axis_size("gz")
    return lax.ppermute(x, "gz", [(i, (i + (2 if i % 2 == 0 else -2)) % n) for i in range(n)])


def shards(phases, diag, local_tiles, local_pairs, face_tiles, face_pairs, layer_tiles, layer_pairs):
    own = layer_tiles.reshape(32, D, D)
    face = face_tiles.reshape(2, 8, D, D)
    own_pairs = layer_pairs.reshape(2, 32)
    fpairs = face_pairs.reshape(2, 2, 8)
    packed, xpack, ypack = pack(own, face)
    low = shift(packed, "gz", 1)
    low_pairs = shift(own_pairs, "gz", 1)
    west_tiles = shift(xpack, "gx", 1)
    west_pairs = shift(fpairs[0], "gx", 1)
    south_tiles = shift(ypack, "gy", 1)
    south_pairs = shift(fpairs[1], "gy", 1)
    *now, south, north, square = initial_vectors(phases.reshape(E, E, D, R))
    odd = lax.rem(lax.axis_index("gz"), 2).astype(jnp.int32).reshape(1)
    local_ops = local_operator(local_pairs.reshape(2, 48), diag.reshape(C, D, D), local_tiles.reshape(48, D, D))
    face_ops = face_operators(fpairs, west_pairs, south_pairs, face, west_tiles, south_tiles)
    layer_ops = layer_operators(odd, own_pairs, low_pairs, own, low)

    sums = [square]
    prev = None
    for step in range(3):
        x = [across(p) for p in now]
        east = shift(now[0], "gx", -1)
        west = shift(now[3], "gx", 1)
        north_in = shift(south, "gy", -1)
        south_in = shift(north, "gy", 1)
        z = [forward(p) for p in x]
        acc = apply_local(local_ops, now)
        acc = apply_faces(face_ops, east, west, north_in, south_in, acc)
        acc = apply_across(layer_ops, x, acc)
        last = step == 2
        out = finish(layer_ops, z, acc, now, prev, 1.0 if step == 0 else 2.0, last)
        sums.append(out[-1])
        if last:
            result = out[0]
        else:
            prev = now
            *now, south, north, _ = out
    partial = jnp.concatenate(sums, axis=0)
    a = lax.psum(lax.psum(partial, "gx"), "gy")
    m = jnp.stack([a[0], a[1], 2.0 * a[2] - a[0], 2.0 * a[3] - a[1], 2.0 * a[4] - a[0], 2.0 * a[5] - a[1], 2.0 * a[6] - a[0]])
    normalizer = lax.axis_size("gx") * lax.axis_size("gy") * C * D
    return (result.reshape(E, E, 1, D, R), (m / normalizer)[None])


def solution(mesh):
    in_specs = (
        P("gx", "gy", "gz", None, None),
        P("gx", "gy", "gz", None, None),
        P("gx", "gy", "gz", None, None, None),
        P("gx", "gy", "gz", None, None),
        P("gx", "gy", "gz", None, None, None, None),
        P("gx", "gy", "gz", None, None, None),
        P("gx", "gy", "gz", None, None, None),
        P("gx", "gy", "gz", None, None),
    )
    out_specs = (P("gx", "gy", "gz", None, None), P("gz", None, None))
    return jax.shard_map(shards, mesh=mesh, in_specs=in_specs, out_specs=out_specs, check_vma=False)
```

```python
import functools
import math

import jax
import jax.numpy as jnp
from jax import lax
from jax.experimental import pallas as pl
from jax.experimental.pallas import tpu as pltpu
from jax.sharding import PartitionSpec as P


D = 96
R = 256
H = 128
E = 4
C = 16
N = C * D
G = E * D
F32 = jnp.float32
BF16 = jnp.bfloat16
B = 192
PARAMS = pltpu.CompilerParams(vmem_limit_bytes=18 << 20)
LIGHT = pltpu.CompilerParams(vmem_limit_bytes=8 << 20)


def vmem():
    return pl.BlockSpec(memory_space=pltpu.VMEM)


def smem():
    return pl.BlockSpec(memory_space=pltpu.SMEM)


def anywhere():
    return pl.BlockSpec(memory_space=pl.ANY)


def cost(flops, moved):
    return pl.CostEstimate(flops=flops, bytes_accessed=moved, transcendentals=0)


def split(x):
    hi = x.astype(BF16)
    return hi, (x - hi.astype(F32)).astype(BF16)


def dot(a, b):
    return jnp.dot(a, b, preferred_element_type=F32)


def rows_of(i, size):
    return pl.ds(pl.multiple_of(i * size, 16), size)


def cosine(x):
    turns = jnp.floor(x * (0.5 / math.pi) + 0.5)
    x = x - turns * (2.0 * math.pi)
    y = x * 0.5
    t = y * y
    s = t * (-1.0 / 39916800.0) + (1.0 / 362880.0)
    s = s * t + (-1.0 / 5040.0)
    s = s * t + (1.0 / 120.0)
    s = s * t + (-1.0 / 6.0)
    s = y + y * t * s
    return 1.0 - 2.0 * s * s


def colsum(x):
    return jnp.sum(x, axis=0, keepdims=True)


def field(n):
    return jax.ShapeDtypeStruct((n, H), F32)


def moment(n):
    return jax.ShapeDtypeStruct((n, H), F32)


def place_faces(i, w, west, east, south, north):
    at = rows_of(lax.shift_right_logical(i, 1), D)
    odd = lax.bitwise_and(i, 1)

    @pl.when(odd == 0)
    def _():
        south[at, :] = w[0:D]

    @pl.when(odd == 1)
    def _():
        north[at, :] = w[D : 2 * D]

    @pl.when(i < 2)
    def _():
        west[rows_of(i, B), :] = w

    @pl.when(i >= 6)
    def _():
        east[rows_of(i - 6, B), :] = w


def initial_body(ph, _, *outs):
    def step(i, carry):
        v = math.sqrt(2.0) * cosine(ph[rows_of(i, B), :])
        sums = []
        for h in range(2):
            out, west, east, south, north, _ = outs[6 * h : 6 * h + 6]
            w = v[:, H * h : H * h + H]
            out[rows_of(i, B), :] = w
            place_faces(i, w, west, east, south, north)
            sums.append(carry[h] + colsum(w * w))
        return tuple(sums)

    zero = jnp.zeros((1, H), F32)
    sums = lax.fori_loop(0, 8, step, (zero, zero))
    for h in range(2):
        outs[6 * h + 5][...] = sums[h]


def initial_vectors(phases, after):
    half = (field(N),) + (field(G),) * 4 + (moment(1),)
    return pl.pallas_call(
        initial_body,
        out_shape=half * 2,
        in_specs=[vmem(), anywhere()],
        out_specs=(vmem(),) * 12,
        compiler_params=LIGHT,
        cost_estimate=cost(30 * N * R, 12 * N * R),
        name="initial",
    )(phases, after)


def pack_body(tiles, _, out):
    def step(j, carry):
        last = tiles[4 * j + 3]
        for i in range(3):
            out[3 * j + i, :, 0:D] = tiles[4 * j + i]
            out[3 * j + i, :, D:128] = last[:, 32 * i : 32 * i + 32]
        return carry

    lax.fori_loop(0, tiles.shape[0] // 4, step, 0)


def pack(tiles, after):
    n = tiles.shape[0]
    return pl.pallas_call(
        pack_body,
        out_shape=jax.ShapeDtypeStruct((3 * n // 4, D, 128), F32),
        in_specs=[vmem(), anywhere()],
        out_specs=vmem(),
        compiler_params=LIGHT,
        cost_estimate=cost(0, 4 * n * D * 256),
        name="pack",
    )(tiles, after)


def unpacked(ref, j, i):
    if i < 3:
        return ref[3 * j + i, :, 0:D]
    parts = [ref[3 * j + n, :, D:128] for n in range(3)]
    return jnp.concatenate(parts, axis=1)


def widened(tile, place):
    wide = jnp.concatenate([tile, jnp.zeros((D, G - D), F32)], axis=1)
    return pltpu.roll(wide, place * D, 1)


def accumulate(acc, row, col, tile):
    group = lax.shift_right_logical(col, 2)
    at = (group, rows_of(row, D), slice(None))
    acc[at] = acc[at] + widened(tile, lax.bitwise_and(col, 3))


def clear(acc):
    def step(i, carry):
        for g in range(4):
            acc[g, rows_of(i, D), :] = jnp.zeros((D, G), F32)
        return carry

    lax.fori_loop(0, C, step, 0)


def emit(acc, put):
    def step(i, carry):
        for g in range(4):
            h, l = split(acc[g, rows_of(i, D), :])
            put((rows_of(i, D), slice(G * g, G * g + G)), h, l)
        return carry

    lax.fori_loop(0, C, step, 0)


def local_body(pairs, diag, tiles, hi, lo, token, acc):
    token[...] = jnp.zeros((8, 128), F32)
    clear(acc)
    for c in range(C):
        t = diag[c]
        acc[c // 4, D * c : D * c + D, D * (c % 4) : D * (c % 4) + D] = t + t.T

    def step(j, carry):
        for i in range(4):
            k = 4 * j + i
            o = pairs[0, k]
            p = pairs[1, k]
            t = tiles[k]
            accumulate(acc, o, p, t)
            accumulate(acc, p, o, t.T)
        return carry

    lax.fori_loop(0, 12, step, 0)

    def put(at, h, l):
        hi[at] = h
        lo[at] = l

    emit(acc, put)


def local_operator(pairs, diag, tiles):
    out = pltpu.VMEM((N, N), BF16)
    return pl.pallas_call(
        local_body,
        out_shape=(out, out, jax.ShapeDtypeStruct((8, 128), F32)),
        in_specs=[smem(), vmem(), vmem()],
        out_specs=(vmem(),) * 3,
        scratch_shapes=[pltpu.VMEM((4, N, G), F32)],
        compiler_params=PARAMS,
        cost_estimate=cost(30 * N * N, 8 * N * N),
        name="local_operator",
    )(pairs, diag, tiles)


def layer_body(odd, own_pairs, low_pairs, own, low, _, hi, lo, token, acc):
    token[...] = jnp.zeros((8, 128), F32)

    def build(slot, carry):
        mine = slot == odd[0]
        clear(acc)

        @pl.when(mine)
        def _():
            def step(j, c):
                for i in range(4):
                    k = 4 * j + i
                    accumulate(acc, own_pairs[0, k], own_pairs[1, k], own[k])
                return c

            lax.fori_loop(0, 8, step, 0)

        @pl.when(jnp.logical_not(mine))
        def _():
            def step(j, c):
                for i in range(4):
                    k = 4 * j + i
                    accumulate(acc, low_pairs[1, k], low_pairs[0, k], unpacked(low, j, i).T)
                return c

            lax.fori_loop(0, 8, step, 0)

        def put(at, h, l):
            hi[(slot,) + at] = h
            lo[(slot,) + at] = l

        emit(acc, put)
        return carry

    lax.fori_loop(0, 2, build, 0)


def layer_operators(odd, own_pairs, low_pairs, own, low, after):
    out = pltpu.VMEM((2, N, N), BF16)
    return pl.pallas_call(
        layer_body,
        out_shape=(out, out, jax.ShapeDtypeStruct((8, 128), F32)),
        in_specs=[smem(), smem(), smem(), vmem(), vmem(), anywhere()],
        out_specs=(vmem(),) * 3,
        scratch_shapes=[pltpu.VMEM((4, N, G), F32)],
        compiler_params=PARAMS,
        cost_estimate=cost(50 * N * N, 16 * N * N),
        name="layer_operators",
    )(odd, own_pairs, low_pairs, own, low, after)


def face_op_body(pairs, west_pairs, south_pairs, face, west, south, _, hi, lo, token, acc):
    token[...] = jnp.zeros((8, 128), F32)
    for i in range(4):
        acc[i] = jnp.zeros((G, G), F32)

    def add(i, row, col, tile):
        at = (i, rows_of(row, D), slice(None))
        acc[at] = acc[at] + widened(tile, col)

    def step(k, carry):
        add(0, pairs[0, 0, k], pairs[0, 1, k], face[0, k])
        add(2, pairs[1, 0, k], pairs[1, 1, k], face[1, k])
        return carry

    lax.fori_loop(0, 8, step, 0)

    def step(j, carry):
        for i in range(4):
            k = 4 * j + i
            add(1, west_pairs[1, k], west_pairs[0, k], unpacked(west, j, i).T)
            add(3, south_pairs[1, k], south_pairs[0, k], unpacked(south, j, i).T)
        return carry

    lax.fori_loop(0, 2, step, 0)

    def step(i, carry):
        h, l = split(acc[i])
        hi[i] = h
        lo[i] = l
        return carry

    lax.fori_loop(0, 4, step, 0)


def face_operators(pairs, west_pairs, south_pairs, face, west, south, after):
    out = pltpu.VMEM((4, G, G), BF16)
    return pl.pallas_call(
        face_op_body,
        out_shape=(out, out, jax.ShapeDtypeStruct((8, 128), F32)),
        in_specs=[smem()] * 3 + [vmem()] * 3 + [anywhere()],
        out_specs=(vmem(),) * 3,
        scratch_shapes=[pltpu.VMEM((4, G, G), F32)],
        compiler_params=PARAMS,
        cost_estimate=cost(40 * G * G, 32 * G * G),
        name="face_operators",
    )(pairs, west_pairs, south_pairs, face, west, south, after)


def load_vector(v, pair):
    def step(i, carry):
        h, l = split(v[rows_of(i, G), :])
        pair[rows_of(i, G), 0:H] = h
        pair[rows_of(i, G), H : 2 * H] = l
        return carry

    lax.fori_loop(0, v.shape[0] // G, step, 0)


def product(hi, lo, pair):
    t = dot(hi, pair[...])
    return t[:, 0:H] + (t[:, H : 2 * H] + dot(lo, pair[:, 0:H]))


PAIR = [pltpu.VMEM((N, 2 * H), BF16)]
PRODUCT_COST = cost(6 * N * N * H, 4 * N * N)


def local_product_body(hi, lo, v, _, out, pair):
    load_vector(v, pair)

    def step(i, carry):
        at = rows_of(i, G)
        out[at, :] = product(hi[at, :], lo[at, :], pair)
        return carry

    lax.fori_loop(0, E, step, 0)


def apply_local(ops, v, after):
    return pl.pallas_call(
        local_product_body,
        out_shape=field(N),
        in_specs=[vmem()] * 3 + [anywhere()],
        out_specs=vmem(),
        scratch_shapes=PAIR,
        compiler_params=LIGHT,
        cost_estimate=PRODUCT_COST,
        name="apply_local",
    )(*ops, v, after)


def across_body(hi, lo, fhi, flo, v, east, west, north, south, acc, _, out, pair, side):
    load_vector(v, pair)

    def step(i, carry):
        at = rows_of(i, G)
        out[at, :] = acc[at, :] + product(hi[0, at, :], lo[0, at, :], pair)
        return carry

    lax.fori_loop(0, E, step, 0)
    for i, face in enumerate((east, west, north, south)):
        h, l = split(face[...])
        side[i, :, 0:H] = h
        side[i, :, H : 2 * H] = l

    def term(i, carry):
        t = product(fhi[i], flo[i], side.at[i])
        along = i < 2
        for s in range(E):
            row = jnp.where(along, s + jnp.where(i == 0, 3 * E, 0), E * s + jnp.where(i == 2, 3, 0))
            at = rows_of(row, D)
            out[at, :] = out[at, :] + t[D * s : D * s + D]
        return carry

    lax.fori_loop(0, 4, term, 0)


def apply_across(ops, face_ops, v, faces, acc, after):
    return pl.pallas_call(
        across_body,
        out_shape=field(N),
        in_specs=[vmem()] * 10 + [anywhere()],
        out_specs=vmem(),
        scratch_shapes=PAIR + [pltpu.VMEM((4, G, 2 * H), BF16)],
        compiler_params=LIGHT,
        cost_estimate=PRODUCT_COST,
        name="apply_across",
    )(*ops, *face_ops, v, *faces, acc, after)


def finish_body(scale, with_prev, last, *refs):
    refs = list(refs)
    hi, lo, z, acc, now = refs[:5]
    refs = refs[5:]
    prev = refs.pop(0) if with_prev else None
    if last == 1:
        refs.pop(0)
    refs.pop(0)
    full, refs = refs[0], refs[1:]
    faces = ()
    if last is None:
        faces, refs = refs[:4], refs[4:]
    mom, pair = refs
    load_vector(z, pair)

    def step(i, carry):
        at = rows_of(i, B)
        w = acc[at, :] + product(hi[1, at, :], lo[1, at, :], pair)
        if scale != 1.0:
            w = scale * w
        if with_prev:
            w = w - prev[at, :]
        full[at, :] = w
        if last is None:
            place_faces(i, w, *faces)
        v = now[at, :]
        return carry[0] + colsum(w * v), carry[1] + colsum(w * w)

    zero = jnp.zeros((1, H), F32)
    cross, square = lax.fori_loop(0, 8, step, (zero, zero))
    mom[0:1, :] = cross
    mom[1:2, :] = square


def finish(ops, z, acc, now, prev, after, scale, last=None, partial=None):
    args = [*ops, z, acc, now]
    if prev is not None:
        args.append(prev)
    in_specs = [vmem()] * len(args)
    aliases = {}
    if last == 1:
        aliases = {len(args): 0}
        args.append(partial)
        in_specs.append(anywhere())
    args.append(after)
    in_specs.append(anywhere())
    if last is None:
        out_shape = (field(N),) + (field(G),) * 4 + (moment(2),)
        out_specs = (vmem(),) * 6
    else:
        out_shape = (jax.ShapeDtypeStruct((N, R), F32), moment(2))
        out_specs = (pl.BlockSpec((N, H), lambda _: (0, last)), pl.BlockSpec((2, H), lambda _: (0, 0)))
    return pl.pallas_call(
        functools.partial(finish_body, scale, prev is not None, last),
        grid=() if last is None else (1,),
        out_shape=out_shape,
        in_specs=in_specs,
        out_specs=out_specs,
        scratch_shapes=PAIR,
        input_output_aliases=aliases,
        compiler_params=LIGHT,
        cost_estimate=PRODUCT_COST,
        name="finish",
    )(*args)


def shift(x, axis, distance):
    n = lax.axis_size(axis)
    return lax.ppermute(x, axis, [(i, (i + distance) % n) for i in range(n)])


def flip(x, axis, bits):
    n = lax.axis_size(axis)
    return lax.ppermute(x, axis, [(i, i ^ bits) for i in range(n)])


def forward(x):
    n = lax.axis_size("gz")
    return lax.ppermute(x, "gz", [(i, (i + (2 if i % 2 == 0 else -2)) % n) for i in range(n)])


def total(x, axis):
    return (x + flip(x, axis, 1)) + (flip(x, axis, 2) + flip(x, axis, 3))


def send(half):
    v, west, east, south, north = half[:5]
    x = flip(v, "gz", 1)
    faces = (
        shift(west, "gx", -1), shift(east, "gx", 1), shift(south, "gy", -1), shift(north, "gy", 1)
    )
    return x, faces


def shards(phases, diag, local_tiles, local_pairs, face_tiles, face_pairs, layer_tiles, layer_pairs):
    own = layer_tiles.reshape(32, D, D)
    face = face_tiles.reshape(2, 8, D, D)
    own_pairs = layer_pairs.reshape(2, 32)
    fpairs = face_pairs.reshape(2, 2, 8)
    packed = pack(own, own_pairs)
    xpack = pack(face[0], packed)
    ypack = pack(face[1], xpack)
    low = shift(packed, "gz", 1)
    low_pairs = shift(own_pairs, "gz", 1)
    west_tiles = shift(xpack, "gx", 1)
    west_pairs = shift(fpairs[0], "gx", 1)
    south_tiles = shift(ypack, "gy", 1)
    south_pairs = shift(fpairs[1], "gy", 1)
    first = initial_vectors(phases.reshape(N, R), ypack)
    halves = [first[:6], first[6:]]
    odd = lax.rem(lax.axis_index("gz"), 2).astype(jnp.int32).reshape(1)
    sums = [[half[5]] for half in halves]
    prev = [None, None]
    sent = [send(halves[0]), send(halves[1])]
    *local_ops, token = local_operator(local_pairs.reshape(2, 48), diag.reshape(C, D, D), local_tiles.reshape(48, D, D))
    *layer_ops, token = layer_operators(odd, own_pairs, low_pairs, own, low, token)
    accs = [None, None]

    result = None
    for step in range(3):
        scale = 1.0 if step == 0 else 2.0
        last = step == 2
        xa, fa = sent[0]
        xb, fb = sent[1]
        xa, token = lax.optimization_barrier((xa, token))
        za = forward(xa)
        if step == 0:
            *face_ops, token = face_operators(fpairs, west_pairs, south_pairs, face, west_tiles, south_tiles, token)
            accs[0] = apply_local(local_ops, halves[0][0], token)
        else:
            accs[1] = apply_local(local_ops, halves[1][0], token)
            token = accs[1]
        acc_a = apply_across(layer_ops, face_ops, xa, fa, accs[0], token)
        if step == 0:
            accs[1] = apply_local(local_ops, halves[1][0], acc_a)
            token = accs[1]
        xb, acc_a, token = lax.optimization_barrier((xb, acc_a, token))
        if step == 0:
            accs[1] = token
        zb = forward(xb)
        out_a = finish(layer_ops, za, acc_a, halves[0][0], prev[0], xb, scale, 0 if last else None)
        sums[0].append(out_a[-1])
        if not last:
            prev[0], halves[0] = halves[0][0], out_a
            sent[0] = send(out_a)
        acc_b = apply_across(layer_ops, face_ops, xb, fb, accs[1], out_a[-1])
        tail = acc_b
        if not last:
            accs[0] = apply_local(local_ops, out_a[0], acc_b)
            tail = accs[0]
        out_b = finish(layer_ops, zb, acc_b, halves[1][0], prev[1], tail, scale, 1 if last else None, out_a[0])
        sums[1].append(out_b[-1])
        if not last:
            prev[1], halves[1] = halves[1][0], out_b
            sent[1] = send(out_b)
            token = out_b[-1]
        else:
            result = out_b[0]
    partial = jnp.concatenate([jnp.concatenate(s, axis=0) for s in sums], axis=1)
    a = total(total(partial, "gx"), "gy")
    m = jnp.stack([a[0], a[1], 2.0 * a[2] - a[0], 2.0 * a[3] - a[1], 2.0 * a[4] - a[0], 2.0 * a[5] - a[1], 2.0 * a[6] - a[0]])
    normalizer = lax.axis_size("gx") * lax.axis_size("gy") * C * D
    return (result.reshape(E, E, 1, D, R), (m / normalizer)[None])


def solution(mesh):
    in_specs = (
        P("gx", "gy", "gz", None, None),
        P("gx", "gy", "gz", None, None),
        P("gx", "gy", "gz", None, None, None),
        P("gx", "gy", "gz", None, None),
        P("gx", "gy", "gz", None, None, None, None),
        P("gx", "gy", "gz", None, None, None),
        P("gx", "gy", "gz", None, None, None),
        P("gx", "gy", "gz", None, None),
    )
    out_specs = (P("gx", "gy", "gz", None, None), P("gz", None, None))
    return jax.shard_map(shards, mesh=mesh, in_specs=in_specs, out_specs=out_specs, check_vma=False)
```

```python
import functools
import math

import jax
import jax.numpy as jnp
from jax import lax
from jax.experimental import pallas as pl
from jax.experimental.pallas import tpu as pltpu
from jax.sharding import PartitionSpec as P


D = 96
R = 256
H = 128
E = 4
C = 16
N = C * D
G = E * D
F32 = jnp.float32
BF16 = jnp.bfloat16
B = 192
PARAMS = pltpu.CompilerParams(vmem_limit_bytes=18 << 20)
LIGHT = pltpu.CompilerParams(vmem_limit_bytes=8 << 20)


def vmem():
    return pl.BlockSpec(memory_space=pltpu.VMEM)


def smem():
    return pl.BlockSpec(memory_space=pltpu.SMEM)


def anywhere():
    return pl.BlockSpec(memory_space=pl.ANY)


def cost(flops, moved):
    return pl.CostEstimate(flops=flops, bytes_accessed=moved, transcendentals=0)


def split(x):
    hi = x.astype(BF16)
    return hi, (x - hi.astype(F32)).astype(BF16)


def dot(a, b):
    return jnp.dot(a, b, preferred_element_type=F32)


def rows_of(i, size):
    return pl.ds(pl.multiple_of(i * size, 16), size)


def cosine(x):
    turns = jnp.floor(x * (0.5 / math.pi) + 0.5)
    x = x - turns * (2.0 * math.pi)
    y = x * 0.5
    t = y * y
    s = t * (-1.0 / 39916800.0) + (1.0 / 362880.0)
    s = s * t + (-1.0 / 5040.0)
    s = s * t + (1.0 / 120.0)
    s = s * t + (-1.0 / 6.0)
    s = y + y * t * s
    return 1.0 - 2.0 * s * s


def colsum(x):
    return jnp.sum(x, axis=0, keepdims=True)


def field(n):
    return jax.ShapeDtypeStruct((n, H), F32)


def moment(n):
    return jax.ShapeDtypeStruct((n, H), F32)


def place_faces(i, w, west, east, south, north):
    at = rows_of(lax.shift_right_logical(i, 1), D)
    odd = lax.bitwise_and(i, 1)

    @pl.when(odd == 0)
    def _():
        south[at, :] = w[0:D]

    @pl.when(odd == 1)
    def _():
        north[at, :] = w[D : 2 * D]

    @pl.when(i < 2)
    def _():
        west[rows_of(i, B), :] = w

    @pl.when(i >= 6)
    def _():
        east[rows_of(i - 6, B), :] = w


def initial_body(ph, _, *outs):
    def step(i, carry):
        v = math.sqrt(2.0) * cosine(ph[rows_of(i, B), :])
        sums = []
        for h in range(2):
            out, west, east, south, north, _ = outs[6 * h : 6 * h + 6]
            w = v[:, H * h : H * h + H]
            out[rows_of(i, B), :] = w
            place_faces(i, w, west, east, south, north)
            sums.append(carry[h] + colsum(w * w))
        return tuple(sums)

    zero = jnp.zeros((1, H), F32)
    sums = lax.fori_loop(0, 8, step, (zero, zero))
    for h in range(2):
        outs[6 * h + 5][...] = sums[h]


def initial_vectors(phases, after):
    half = (field(N),) + (field(G),) * 4 + (moment(1),)
    return pl.pallas_call(
        initial_body,
        out_shape=half * 2,
        in_specs=[vmem(), anywhere()],
        out_specs=(vmem(),) * 12,
        compiler_params=LIGHT,
        cost_estimate=cost(30 * N * R, 12 * N * R),
        name="initial",
    )(phases, after)


def pack_body(tiles, _, out):
    def step(j, carry):
        last = tiles[4 * j + 3]
        for i in range(3):
            out[3 * j + i, :, 0:D] = tiles[4 * j + i]
            out[3 * j + i, :, D:128] = last[:, 32 * i : 32 * i + 32]
        return carry

    lax.fori_loop(0, tiles.shape[0] // 4, step, 0)


def pack(tiles, after):
    n = tiles.shape[0]
    return pl.pallas_call(
        pack_body,
        out_shape=jax.ShapeDtypeStruct((3 * n // 4, D, 128), F32),
        in_specs=[vmem(), anywhere()],
        out_specs=vmem(),
        compiler_params=LIGHT,
        cost_estimate=cost(0, 4 * n * D * 256),
        name="pack",
    )(tiles, after)


def unpacked(ref, j, i):
    if i < 3:
        return ref[3 * j + i, :, 0:D]
    parts = [ref[3 * j + n, :, D:128] for n in range(3)]
    return jnp.concatenate(parts, axis=1)


def widened(tile, place):
    wide = jnp.concatenate([tile, jnp.zeros((D, G - D), F32)], axis=1)
    return pltpu.roll(wide, place * D, 1)


def accumulate(acc, row, col, tile):
    group = lax.shift_right_logical(col, 2)
    at = (group, rows_of(row, D), slice(None))
    acc[at] = acc[at] + widened(tile, lax.bitwise_and(col, 3))


def clear(acc):
    def step(i, carry):
        for g in range(4):
            acc[g, rows_of(i, D), :] = jnp.zeros((D, G), F32)
        return carry

    lax.fori_loop(0, C, step, 0)


def emit(acc, put):
    def step(i, carry):
        for g in range(4):
            h, l = split(acc[g, rows_of(i, D), :])
            put((rows_of(i, D), slice(G * g, G * g + G)), h, l)
        return carry

    lax.fori_loop(0, C, step, 0)


def local_body(pairs, diag, tiles, hi, lo, token, acc):
    token[...] = jnp.zeros((8, 128), F32)
    clear(acc)
    for c in range(C):
        t = diag[c]
        acc[c // 4, D * c : D * c + D, D * (c % 4) : D * (c % 4) + D] = t + t.T

    def step(j, carry):
        for i in range(4):
            k = 4 * j + i
            o = pairs[0, k]
            p = pairs[1, k]
            t = tiles[k]
            accumulate(acc, o, p, t)
            accumulate(acc, p, o, t.T)
        return carry

    lax.fori_loop(0, 12, step, 0)

    def put(at, h, l):
        hi[at] = h
        lo[at] = l

    emit(acc, put)


def local_operator(pairs, diag, tiles):
    out = pltpu.VMEM((N, N), BF16)
    return pl.pallas_call(
        local_body,
        out_shape=(out, out, jax.ShapeDtypeStruct((8, 128), F32)),
        in_specs=[smem(), vmem(), vmem()],
        out_specs=(vmem(),) * 3,
        scratch_shapes=[pltpu.VMEM((4, N, G), F32)],
        compiler_params=PARAMS,
        cost_estimate=cost(30 * N * N, 8 * N * N),
        name="local_operator",
    )(pairs, diag, tiles)


def layer_body(odd, own_pairs, low_pairs, own, low, _, hi, lo, token, acc):
    token[...] = jnp.zeros((8, 128), F32)

    def build(slot, carry):
        mine = slot == odd[0]
        clear(acc)

        @pl.when(mine)
        def _():
            def step(j, c):
                for i in range(4):
                    k = 4 * j + i
                    accumulate(acc, own_pairs[0, k], own_pairs[1, k], own[k])
                return c

            lax.fori_loop(0, 8, step, 0)

        @pl.when(jnp.logical_not(mine))
        def _():
            def step(j, c):
                for i in range(4):
                    k = 4 * j + i
                    accumulate(acc, low_pairs[1, k], low_pairs[0, k], unpacked(low, j, i).T)
                return c

            lax.fori_loop(0, 8, step, 0)

        def put(at, h, l):
            hi[(slot,) + at] = h
            lo[(slot,) + at] = l

        emit(acc, put)
        return carry

    lax.fori_loop(0, 2, build, 0)


def layer_operators(odd, own_pairs, low_pairs, own, low, after):
    out = pltpu.VMEM((2, N, N), BF16)
    return pl.pallas_call(
        layer_body,
        out_shape=(out, out, jax.ShapeDtypeStruct((8, 128), F32)),
        in_specs=[smem(), smem(), smem(), vmem(), vmem(), anywhere()],
        out_specs=(vmem(),) * 3,
        scratch_shapes=[pltpu.VMEM((4, N, G), F32)],
        compiler_params=PARAMS,
        cost_estimate=cost(50 * N * N, 16 * N * N),
        name="layer_operators",
    )(odd, own_pairs, low_pairs, own, low, after)


def face_op_body(pairs, west_pairs, south_pairs, face, west, south, _, hi, lo, token, acc):
    token[...] = jnp.zeros((8, 128), F32)
    for i in range(4):
        acc[i] = jnp.zeros((G, G), F32)

    def add(i, row, col, tile):
        at = (i, rows_of(row, D), slice(None))
        acc[at] = acc[at] + widened(tile, col)

    def step(k, carry):
        add(0, pairs[0, 0, k], pairs[0, 1, k], face[0, k])
        add(2, pairs[1, 0, k], pairs[1, 1, k], face[1, k])
        return carry

    lax.fori_loop(0, 8, step, 0)

    def step(j, carry):
        for i in range(4):
            k = 4 * j + i
            add(1, west_pairs[1, k], west_pairs[0, k], unpacked(west, j, i).T)
            add(3, south_pairs[1, k], south_pairs[0, k], unpacked(south, j, i).T)
        return carry

    lax.fori_loop(0, 2, step, 0)

    def step(i, carry):
        h, l = split(acc[i])
        hi[i] = h
        lo[i] = l
        return carry

    lax.fori_loop(0, 4, step, 0)


def face_operators(pairs, west_pairs, south_pairs, face, west, south, after):
    out = pltpu.VMEM((4, G, G), BF16)
    return pl.pallas_call(
        face_op_body,
        out_shape=(out, out, jax.ShapeDtypeStruct((8, 128), F32)),
        in_specs=[smem()] * 3 + [vmem()] * 3 + [anywhere()],
        out_specs=(vmem(),) * 3,
        scratch_shapes=[pltpu.VMEM((4, G, G), F32)],
        compiler_params=PARAMS,
        cost_estimate=cost(40 * G * G, 32 * G * G),
        name="face_operators",
    )(pairs, west_pairs, south_pairs, face, west, south, after)


def load_vector(v, pair):
    def step(i, carry):
        h, l = split(v[rows_of(i, G), :])
        pair[rows_of(i, G), 0:H] = h
        pair[rows_of(i, G), H : 2 * H] = l
        return carry

    lax.fori_loop(0, v.shape[0] // G, step, 0)


def product(hi, lo, pair):
    t = dot(hi, pair[...])
    return t[:, 0:H] + (t[:, H : 2 * H] + dot(lo, pair[:, 0:H]))


PAIR = [pltpu.VMEM((N, 2 * H), BF16)]
PRODUCT_COST = cost(6 * N * N * H, 4 * N * N)


def local_product_body(hi, lo, v, _, out, pair):
    load_vector(v, pair)

    def step(i, carry):
        at = rows_of(i, G)
        out[at, :] = product(hi[at, :], lo[at, :], pair)
        return carry

    lax.fori_loop(0, E, step, 0)


def apply_local(ops, v, after):
    return pl.pallas_call(
        local_product_body,
        out_shape=field(N),
        in_specs=[vmem()] * 3 + [anywhere()],
        out_specs=vmem(),
        scratch_shapes=PAIR,
        compiler_params=LIGHT,
        cost_estimate=PRODUCT_COST,
        name="apply_local",
    )(*ops, v, after)


def across_body(hi, lo, fhi, flo, v, east, west, north, south, acc, _, out, pair, side):
    load_vector(v, pair)

    def step(i, carry):
        at = rows_of(i, G)
        out[at, :] = acc[at, :] + product(hi[0, at, :], lo[0, at, :], pair)
        return carry

    lax.fori_loop(0, E, step, 0)
    for i, face in enumerate((east, west, north, south)):
        h, l = split(face[...])
        side[i, :, 0:H] = h
        side[i, :, H : 2 * H] = l

    def term(i, carry):
        t = product(fhi[i], flo[i], side.at[i])
        along = i < 2
        for s in range(E):
            row = jnp.where(along, s + jnp.where(i == 0, 3 * E, 0), E * s + jnp.where(i == 2, 3, 0))
            at = rows_of(row, D)
            out[at, :] = out[at, :] + t[D * s : D * s + D]
        return carry

    lax.fori_loop(0, 4, term, 0)


def apply_across(ops, face_ops, v, faces, acc, after):
    return pl.pallas_call(
        across_body,
        out_shape=field(N),
        in_specs=[vmem()] * 10 + [anywhere()],
        out_specs=vmem(),
        scratch_shapes=PAIR + [pltpu.VMEM((4, G, 2 * H), BF16)],
        compiler_params=LIGHT,
        cost_estimate=PRODUCT_COST,
        name="apply_across",
    )(*ops, *face_ops, v, *faces, acc, after)


def finish_body(scale, with_prev, last, *refs):
    refs = list(refs)
    hi, lo, z, acc, now = refs[:5]
    refs = refs[5:]
    prev = refs.pop(0) if with_prev else None
    if last == 1:
        refs.pop(0)
    refs.pop(0)
    full, refs = refs[0], refs[1:]
    faces = ()
    if last is None:
        faces, refs = refs[:4], refs[4:]
    mom, pair = refs
    load_vector(z, pair)

    def step(i, carry):
        at = rows_of(i, B)
        w = acc[at, :] + product(hi[1, at, :], lo[1, at, :], pair)
        if scale != 1.0:
            w = scale * w
        if with_prev:
            w = w - prev[at, :]
        full[at, :] = w
        if last is None:
            place_faces(i, w, *faces)
        v = now[at, :]
        return carry[0] + colsum(w * v), carry[1] + colsum(w * w)

    zero = jnp.zeros((1, H), F32)
    cross, square = lax.fori_loop(0, 8, step, (zero, zero))
    mom[0:1, :] = cross
    mom[1:2, :] = square


def finish(ops, z, acc, now, prev, after, scale, last=None, partial=None):
    args = [*ops, z, acc, now]
    if prev is not None:
        args.append(prev)
    in_specs = [vmem()] * len(args)
    aliases = {}
    if last == 1:
        aliases = {len(args): 0}
        args.append(partial)
        in_specs.append(anywhere())
    args.append(after)
    in_specs.append(anywhere())
    if last is None:
        out_shape = (field(N),) + (field(G),) * 4 + (moment(2),)
        out_specs = (vmem(),) * 6
    else:
        out_shape = (jax.ShapeDtypeStruct((N, R), F32), moment(2))
        out_specs = (pl.BlockSpec((N, H), lambda _: (0, last)), pl.BlockSpec((2, H), lambda _: (0, 0)))
    return pl.pallas_call(
        functools.partial(finish_body, scale, prev is not None, last),
        grid=() if last is None else (1,),
        out_shape=out_shape,
        in_specs=in_specs,
        out_specs=out_specs,
        scratch_shapes=PAIR,
        input_output_aliases=aliases,
        compiler_params=LIGHT,
        cost_estimate=PRODUCT_COST,
        name="finish",
    )(*args)


def shift(x, axis, distance):
    n = lax.axis_size(axis)
    return lax.ppermute(x, axis, [(i, (i + distance) % n) for i in range(n)])


def flip(x, axis, bits):
    n = lax.axis_size(axis)
    return lax.ppermute(x, axis, [(i, i ^ bits) for i in range(n)])


def forward(x):
    n = lax.axis_size("gz")
    return lax.ppermute(x, "gz", [(i, (i + (2 if i % 2 == 0 else -2)) % n) for i in range(n)])


def total(x, axis):
    return (x + flip(x, axis, 1)) + (flip(x, axis, 2) + flip(x, axis, 3))


def send(half):
    v, west, east, south, north = half[:5]
    x = flip(v, "gz", 1)
    faces = (
        shift(west, "gx", -1), shift(east, "gx", 1), shift(south, "gy", -1), shift(north, "gy", 1)
    )
    return x, faces


def shards(phases, diag, local_tiles, local_pairs, face_tiles, face_pairs, layer_tiles, layer_pairs):
    own = layer_tiles.reshape(32, D, D)
    face = face_tiles.reshape(2, 8, D, D)
    own_pairs = layer_pairs.reshape(2, 32)
    fpairs = face_pairs.reshape(2, 2, 8)
    packed = pack(own, own_pairs)
    xpack = pack(face[0], packed)
    ypack = pack(face[1], xpack)
    low = shift(packed, "gz", 1)
    low_pairs = shift(own_pairs, "gz", 1)
    west_tiles = shift(xpack, "gx", 1)
    west_pairs = shift(fpairs[0], "gx", 1)
    south_tiles = shift(ypack, "gy", 1)
    south_pairs = shift(fpairs[1], "gy", 1)
    first = initial_vectors(phases.reshape(N, R), ypack)
    halves = [first[:6], first[6:]]
    odd = lax.rem(lax.axis_index("gz"), 2).astype(jnp.int32).reshape(1)
    sums = [[half[5]] for half in halves]
    prev = [None, None]
    sent = [send(halves[0]), send(halves[1])]
    *local_ops, token = local_operator(local_pairs.reshape(2, 48), diag.reshape(C, D, D), local_tiles.reshape(48, D, D))
    *layer_ops, token = layer_operators(odd, own_pairs, low_pairs, own, low, token)
    accs = [None, None]

    result = None
    for step in range(3):
        scale = 1.0 if step == 0 else 2.0
        last = step == 2
        xa, fa = sent[0]
        xb, fb = sent[1]
        xa, token = lax.optimization_barrier((xa, token))
        za = forward(xa)
        if step == 0:
            *face_ops, token = face_operators(fpairs, west_pairs, south_pairs, face, west_tiles, south_tiles, token)
            accs[0] = apply_local(local_ops, halves[0][0], token)
        else:
            accs[0] = apply_local(local_ops, halves[0][0], token)
            accs[1] = apply_local(local_ops, halves[1][0], accs[0])
            token = accs[1]
        acc_a = apply_across(layer_ops, face_ops, xa, fa, accs[0], token)
        if step == 0:
            accs[1] = apply_local(local_ops, halves[1][0], acc_a)
            token = accs[1]
        xb, acc_a, token = lax.optimization_barrier((xb, acc_a, token))
        if step == 0:
            accs[1] = token
        zb = forward(xb)
        out_a = finish(layer_ops, za, acc_a, halves[0][0], prev[0], xb, scale, 0 if last else None)
        sums[0].append(out_a[-1])
        if not last:
            prev[0], halves[0] = halves[0][0], out_a
            sent[0] = send(out_a)
        acc_b = apply_across(layer_ops, face_ops, xb, fb, accs[1], out_a[-1])
        tail = acc_b
        out_b = finish(layer_ops, zb, acc_b, halves[1][0], prev[1], tail, scale, 1 if last else None, out_a[0])
        sums[1].append(out_b[-1])
        if not last:
            prev[1], halves[1] = halves[1][0], out_b
            sent[1] = send(out_b)
            token = out_b[-1]
        else:
            result = out_b[0]
    partial = jnp.concatenate([jnp.concatenate(s, axis=0) for s in sums], axis=1)
    a = total(total(partial, "gx"), "gy")
    m = jnp.stack([a[0], a[1], 2.0 * a[2] - a[0], 2.0 * a[3] - a[1], 2.0 * a[4] - a[0], 2.0 * a[5] - a[1], 2.0 * a[6] - a[0]])
    normalizer = lax.axis_size("gx") * lax.axis_size("gy") * C * D
    return (result.reshape(E, E, 1, D, R), (m / normalizer)[None])


def solution(mesh):
    in_specs = (
        P("gx", "gy", "gz", None, None),
        P("gx", "gy", "gz", None, None),
        P("gx", "gy", "gz", None, None, None),
        P("gx", "gy", "gz", None, None),
        P("gx", "gy", "gz", None, None, None, None),
        P("gx", "gy", "gz", None, None, None),
        P("gx", "gy", "gz", None, None, None),
        P("gx", "gy", "gz", None, None),
    )
    out_specs = (P("gx", "gy", "gz", None, None), P("gz", None, None))
    return jax.shard_map(shards, mesh=mesh, in_specs=in_specs, out_specs=out_specs, check_vma=False)
```
